32 devices in a mesh: pts: 2 (over core), cen: 16 (over z, y, x).
Axes of the slice: x: 2, y: 2, z: 4, core: 2. Of those that a mesh axis runs over, the one named last changes fastest.
Arguments:
- points: bfloat16 [2, 1024, 256], P(None, ('pts', 'cen')), may hold values from -4096 to 4096, as said below
- centroids: float32 [16384, 256], P('cen'), may hold values from -6 to 6, as said below
Outputs:
- new_centroids: float32 [16384, 256], P('cen')
- energy: float32 [2, 1024], P(None, 'pts')
The draws below stay inside these ranges and needn't reach their ends.
Inputs may be any that keep to these rules, and one draw needn't show every extreme that they name: Real-valued points. Real-valued centroids.
All inputs are finite; a program needn't handle non-finite values.
Results may differ from the reference program's by a relative error of at most 0.0003.
The reference program's roundings to bfloat16 on the way count: a program that leaves them out, or rounds other values in their place, can miss the bound.
Values may be sent and summed in bfloat16 or wider, within the bound.
A program may use at most 64 MiB of HBM per device.

```python
import jax
import jax.numpy as jnp
from jax import lax

D = 256
PTS_DEV = 32
STEPS = 2
K = 16384
BATCH = 1024
N_CEN = 16


def centroid_table(key):
    return jax.random.normal(jax.random.fold_in(key, 11), (K, D), jnp.float32)


def draw_centroids(key, part):
    return jnp.clip(centroid_table(key), -6.0, 6.0)


def draw_points(key, part):
    base = jax.random.normal(jax.random.fold_in(key, 23), (STEPS, BATCH, D), jnp.float32)
    table = jnp.clip(centroid_table(key), -6.0, 6.0)
    picks = jax.random.randint(jax.random.fold_in(key, 31), (STEPS, BATCH), 0, K)
    order = jnp.arange(BATCH)
    target = (150.0 + 100.0 * (order % 3)).astype(jnp.float32)
    noise = 0.1
    chosen = order % 61 == 0
    picked = table[picks]
    norm_sq = jnp.sum(picked * picked, axis=2)
    strength = 0.5 * (32.0 * target[None, :] / norm_sq + 1.0)
    aligned = picked * strength[:, :, None] + noise * base
    base = jnp.where(chosen[None, :, None], aligned, base)
    return jnp.clip(base, -4096.0, 4096.0).astype(jnp.bfloat16)


def setup_inputs(seed: int = 0) -> dict:
    keys = jax.random.split(jax.random.key(seed), 3)
    points = draw_points(jax.random.fold_in(keys[2], 71), 0)
    centroids = draw_centroids(jax.random.fold_in(keys[2], 71), 0)
    return dict(points=points, centroids=centroids)


TEMPER = 32.0


def reference(points, centroids):
    current = centroids
    energies = []
    for iteration in range(STEPS):
        cent_low = current.astype(jnp.bfloat16)
        cent_sq = jnp.sum(current * current, axis=1)
        blocks = points[iteration].reshape(BATCH // (PTS_DEV * N_CEN), PTS_DEV * N_CEN, D)

        def one_block(carry, rows_blk):
            sums, counts = carry
            inner = lax.dot_general(rows_blk, cent_low, (((1,), (1,)), ((), ())), preferred_element_type=jnp.float32)
            logits = (2.0 * inner - cent_sq[None, :]) / TEMPER
            top = jnp.max(logits, axis=1)
            weights = jnp.exp(logits - top[:, None])
            total = jnp.sum(weights, axis=1)
            resp = weights / total[:, None]
            counts = counts + jnp.sum(resp, axis=0)
            sums = sums + lax.dot_general(resp.astype(jnp.bfloat16), rows_blk, (((0,), (0,)), ((), ())), preferred_element_type=jnp.float32)
            return (sums, counts), top + jnp.log(total)

        start_carry = (jnp.zeros((K, D), jnp.float32), jnp.zeros((K,), jnp.float32))
        (sums, counts), block_energy = lax.scan(one_block, start_carry, blocks)
        current = (current + sums) / (1.0 + counts)[:, None]
        energies.append(block_energy.reshape(BATCH))
    return current, jnp.stack(energies)
```

```python
import functools

import jax
import jax.numpy as jnp
from jax import lax
from jax.experimental import pallas as pl
from jax.experimental.pallas import tpu as pltpu
from jax.sharding import PartitionSpec as P

TEMPER = 32.0
MESH = pl.DeviceIdType.MESH
LANES = 128
ROWS = 256


def split(n):
    near = 1
    while near * near * 4 <= n:
        near *= 2
    assert n % near == 0 and (n // near) & (n // near - 1) == 0
    return n // near, near


def flips(i, n):
    steps, bit = [], 1
    while bit < n:
        steps.append((bit, bit - 2 * bit * lax.rem(i // bit, 2)))
        bit *= 2
    peers = []
    for d in range(n):
        peer = i
        for bit, step in steps:
            if d & bit:
                peer = peer + step
        peers.append(peer)
    return peers


def kernel(far, near, n_pts, pts_ref, cen_ref, out_ref, en_ref,
           x_ref, w_ref, cur_ref, low_ref, sq_ref, tops, stat, got,
           p_send, f_recv, n_recv, s_send, s_recv, c_send, c_recv,
           in_sem, cen_sem):
    steps, own, dim = pts_ref.shape
    k_loc = cen_ref.shape[0]
    n_blk = k_loc // ROWS
    n_cen = far * near
    width = near * own
    cols = width // LANES
    groups = far * cols
    cen = lax.axis_index("cen")
    p = lax.axis_index("pts")
    a = cen // near
    b = lax.rem(cen, near)
    a_flip = flips(a, far)
    b_flip = flips(b, near)
    pts_peers = [lax.rem(p + d, n_pts) for d in range(1, n_pts)]

    barrier = pltpu.get_barrier_semaphore()
    for peer in a_flip[1:]:
        pl.semaphore_signal(barrier, inc=1, device_id={"cen": peer * near + b}, device_id_type=MESH)
    for peer in b_flip[1:]:
        pl.semaphore_signal(barrier, inc=1, device_id={"cen": a * near + peer}, device_id_type=MESH)
    for peer in pts_peers:
        pl.semaphore_signal(barrier, inc=1, device_id={"pts": peer}, device_id_type=MESH)

    def rows_of(blk):
        return pl.ds(pl.multiple_of(blk * ROWS, ROWS), ROWS)

    def lowered(value):
        sq = jnp.sum(value * value, axis=1, keepdims=True) * (1.0 / TEMPER)
        return (value * (2.0 / TEMPER)).astype(jnp.bfloat16), sq

    def cen_copy(blk):
        rows = rows_of(blk)
        return pltpu.make_async_copy(cen_ref.at[rows, :], cur_ref.at[rows, :], cen_sem.at[blk])

    def chunk(s, i, j):
        return x_ref.at[s, pl.ds(pl.multiple_of((i * near + j) * own, own), own), :]

    def pts_copy(s):
        return pltpu.make_async_copy(pts_ref.at[s], chunk(s, a, b), in_sem.at[s])

    def landed(ref, sem):
        pltpu.make_async_remote_copy(
            src_ref=ref, dst_ref=ref, send_sem=sem, recv_sem=sem,
            device_id={"cen": cen}, device_id_type=MESH).wait_recv()

    def sent(ref, sem):
        pltpu.make_async_remote_copy(
            src_ref=ref, dst_ref=ref, send_sem=sem, recv_sem=sem,
            device_id={"cen": cen}, device_id_type=MESH).wait_send()

    def chunks(s, n):
        return x_ref.at[s, pl.ds(0, n * own), :]

    def far_sem(s, i):
        return f_recv.at[i if s == 0 else far + s - 1]

    def near_sem(s, i):
        return n_recv.at[i if s == 0 else far + s - 1]

    def far_copy(s, d):
        return pltpu.make_async_remote_copy(
            src_ref=pts_ref.at[s], dst_ref=chunk(s, a, b),
            send_sem=p_send.at[s], recv_sem=far_sem(s, a),
            device_id={"cen": a_flip[d] * near + b}, device_id_type=MESH)

    def near_copy(s, i, d, src):
        return pltpu.make_async_remote_copy(
            src_ref=src, dst_ref=chunk(s, i, b),
            send_sem=p_send.at[s], recv_sem=near_sem(s, i),
            device_id={"cen": a * near + b_flip[d]}, device_id_type=MESH)

    def send_own(s):
        for d in reversed(range(1, far)):
            far_copy(s, d).start()
        for d in reversed(range(1, near)):
            near_copy(s, a, d, pts_ref.at[s]).start()

    def forward(s):
        if s > 0:
            landed(chunks(s, far - 1), far_sem(s, 0))
        for d in range(1, far):
            i = a_flip[d]
            if s == 0:
                landed(chunk(s, i, b), far_sem(s, i))
            for e in reversed(range(1, near)):
                near_copy(s, i, e, chunk(s, i, b)).start()

    def stat_copy(s, d):
        return pltpu.make_async_remote_copy(
            src_ref=stat.at[s, cen], dst_ref=stat.at[s, cen],
            send_sem=s_send.at[s], recv_sem=s_recv.at[s],
            device_id={"cen": a_flip[d // near] * near + b_flip[d % near]}, device_id_type=MESH)

    def sums_copy(s, d, blk):
        return pltpu.make_async_remote_copy(
            src_ref=got.at[s, p, blk], dst_ref=got.at[s, p, blk],
            send_sem=c_send.at[s], recv_sem=c_recv.at[s, blk],
            device_id={"pts": pts_peers[d - 1]}, device_id_type=MESH)

    for s in range(steps):
        pts_copy(s).start()

    @pl.loop(0, n_blk)
    def _(blk):
        cen_copy(blk).start()

    with jax.named_scope("entry"):
        pl.semaphore_wait(barrier, (far - 1) + (near - 1) + (n_pts - 1))
        send_own(0)

    with jax.named_scope("prepare"):
        @pl.loop(0, n_blk)
        def _(blk):
            cen_copy(blk).wait()
            rows = rows_of(blk)
            low_ref[rows, :], sq = lowered(cur_ref[rows, :])
            sq_ref[rows, :] = jnp.broadcast_to(sq, (ROWS, LANES))

    with jax.named_scope("forward0"):
        forward(0)
    if steps > 1:
        send_own(1)
    for s in range(steps):
        pts_copy(s).wait()

    def one_group(i):
        landed(chunks(0, near - 1), near_sem(0, i))
        for j in range(cols):
            g = i * cols + j
            xg = x_ref[0, pl.ds(pl.multiple_of(g * LANES, LANES), LANES), :]
            logits = lax.dot_general(
                low_ref[...], xg, (((1,), (1,)), ((), ())),
                preferred_element_type=jnp.float32) - sq_ref[...]
            top = jnp.max(logits, axis=0, keepdims=True)
            weights = jnp.exp(logits - top)
            w_ref[:, pl.ds(pl.multiple_of(g * LANES, LANES), LANES)] = weights
            tops[pl.ds(g, 1), :] = top
            stat[0, cen, pl.ds(g, 1), :] = top + jnp.log(jnp.sum(weights, axis=0, keepdims=True))

    for d in range(far):
        with jax.named_scope("group" + str(d)):
            one_group(a_flip[d])

    for s in range(steps):
        for d in reversed(range(1, n_cen)):
            stat_copy(s, d).start()
        if s + 1 < steps:
            with jax.named_scope("forward1"):
                forward(s + 1)
            if s + 2 < steps:
                send_own(s + 2)
        with jax.named_scope("stats" + str(s)):
            landed(stat.at[s, pl.ds(0, n_cen - 1)], s_recv.at[s])
        parts = stat[s]
        best = jnp.max(parts, axis=0)
        energy = best + jnp.log(jnp.sum(jnp.exp(parts - best[None]), axis=0))
        scale = jnp.exp(tops[...] - energy)
        for g in range(groups):
            en_ref[s:s + 1, g * LANES:(g + 1) * LANES] = energy[g:g + 1, :]
        scale = jnp.concatenate([scale[g:g + 1, :] for g in range(groups)], axis=1)

        with jax.named_scope("sums" + str(s)):
            @pl.loop(0, n_blk)
            def _(blk):
                resp = w_ref[rows_of(blk), :] * scale
                part = resp[:, :LANES]
                for g in range(1, groups):
                    part = part + resp[:, g * LANES:(g + 1) * LANES]
                count = jnp.sum(jnp.transpose(part), axis=0, keepdims=True)
                sums = lax.dot_general(
                    resp.astype(jnp.bfloat16), x_ref[s], (((1,), (0,)), ((), ())),
                    preferred_element_type=jnp.float32)
                got[s, p, blk, :ROWS, :] = sums
                got[s, p, blk, ROWS:ROWS + 1, :] = count
                for d in range(1, n_pts):
                    sums_copy(s, d, blk).start()

        if s + 1 < steps:
            landed(chunks(s + 1, far * (near - 1)), near_sem(s + 1, 0))

        def finish(blk, top):
            rows = rows_of(blk)
            landed(got.at[s, pl.ds(0, n_pts - 1), blk], c_recv.at[s, blk])
            sums = got[s, 0, blk, :ROWS, :]
            count = got[s, 0, blk, ROWS:ROWS + 1, :]
            for i in range(1, n_pts):
                sums = sums + got[s, i, blk, :ROWS, :]
                count = count + got[s, i, blk, ROWS:ROWS + 1, :]
            column = jnp.transpose(jnp.broadcast_to(1.0 / (1.0 + count), (LANES, ROWS)))
            column = jnp.concatenate([column] * (dim // LANES), axis=1)
            value = (cur_ref[rows, :] + sums) * column
            if s + 1 == steps:
                out_ref[rows, :] = value
                return top
            cur_ref[rows, :] = value
            low, sq = lowered(value)
            logits = lax.dot_general(
                low, x_ref[s + 1], (((1,), (1,)), ((), ())),
                preferred_element_type=jnp.float32) - sq
            w_ref[rows, :] = logits
            return jnp.maximum(top, jnp.max(logits, axis=0, keepdims=True))

        def weigh(top, blk, total):
            rows = rows_of(blk)
            weights = jnp.exp(w_ref[rows, :] - top)
            w_ref[rows, :] = weights
            return total + jnp.sum(weights, axis=0, keepdims=True)

        with jax.named_scope("finish" + str(s)):
            top = lax.fori_loop(0, n_blk, finish, jnp.full((1, groups * LANES), -jnp.inf, jnp.float32))
        if s + 1 < steps:
            with jax.named_scope("weigh"):
                total = lax.fori_loop(0, n_blk, functools.partial(weigh, top), jnp.zeros_like(top))
            part = top + jnp.log(total)
            for g in range(groups):
                tops[g:g + 1, :] = top[:, g * LANES:(g + 1) * LANES]
                stat[s + 1, cen, g:g + 1, :] = part[:, g * LANES:(g + 1) * LANES]

    with jax.named_scope("drain"):
        for s in range(steps):
            sent(chunks(s, n_cen - 1), p_send.at[s])
            sent(stat.at[s, pl.ds(0, n_cen - 1)], s_send.at[s])
            sent(got.at[s, pl.ds(0, n_pts - 1)], c_send.at[s])


def emit(value_ref, part_ref, out_ref, en_ref, sems):
    copies = [pltpu.make_async_copy(value_ref, out_ref, sems.at[0]),
              pltpu.make_async_copy(part_ref, en_ref, sems.at[1])]
    for copy in copies:
        copy.start()
    for copy in copies:
        copy.wait()


def on_device(far, near, n_pts, points, centroids):
    steps, own, dim = points.shape
    k_loc = centroids.shape[0]
    n_blk = k_loc // ROWS
    n_cen = far * near
    batch = n_cen * own
    groups = batch // LANES
    vmem = pl.BlockSpec(memory_space=pltpu.VMEM)
    dma = pltpu.SemaphoreType.DMA
    value, energy = pl.pallas_call(
        functools.partial(kernel, far, near, n_pts),
        out_shape=(pltpu.VMEM((k_loc, dim), jnp.float32),
                   pltpu.VMEM((steps, batch), jnp.float32)),
        in_specs=[pl.BlockSpec(memory_space=pl.ANY)] * 2,
        out_specs=(vmem, vmem),
        scratch_shapes=[
            pltpu.VMEM((steps, batch, dim), jnp.bfloat16),
            pltpu.VMEM((k_loc, batch), jnp.float32),
            pltpu.VMEM((k_loc, dim), jnp.float32),
            pltpu.VMEM((k_loc, dim), jnp.bfloat16),
            pltpu.VMEM((k_loc, LANES), jnp.float32),
            pltpu.VMEM((groups, LANES), jnp.float32),
            pltpu.VMEM((steps, n_cen, groups, LANES), jnp.float32),
            pltpu.VMEM((steps, n_pts, n_blk, ROWS + 8, dim), jnp.float32),
            dma((steps,)),
            dma((far + steps - 1,)),
            dma((far + steps - 1,)),
            dma((steps,)),
            dma((steps,)),
            dma((steps,)),
            dma((steps, n_blk)),
            dma((steps,)),
            dma((n_blk,)),
        ],
        compiler_params=pltpu.CompilerParams(
            collective_id=0, has_side_effects=True, vmem_limit_bytes=58 * 1024 * 1024),
    )(points, centroids)
    return pl.pallas_call(
        emit,
        out_shape=(jax.ShapeDtypeStruct((k_loc, dim), jnp.float32),
                   jax.ShapeDtypeStruct((steps, batch), jnp.float32)),
        in_specs=[vmem, vmem],
        out_specs=[pl.BlockSpec(memory_space=pltpu.HBM)] * 2,
        scratch_shapes=[dma((2,))],
        compiler_params=pltpu.CompilerParams(vmem_limit_bytes=1024 * 1024),
    )(value, energy)


def solution(mesh):
    far, near = split(mesh.shape["cen"])
    placed = (P(None, ("pts", "cen"), None), P("cen", None))
    return jax.shard_map(
        functools.partial(on_device, far, near, mesh.shape["pts"]),
        mesh=mesh,
        in_specs=placed,
        out_specs=(P("cen", None), P(None, "pts")),
        check_vma=False,
    )
```

```python
import functools

import jax
import jax.numpy as jnp
from jax import lax
from jax.experimental import pallas as pl
from jax.experimental.pallas import tpu as pltpu
from jax.sharding import PartitionSpec as P

TEMPER = 32.0
MESH = pl.DeviceIdType.MESH
LANES = 128
ROWS = 256
BLOCK = 128
UNROLL = 32


def split(n):
    near = 1
    while near * near * 4 <= n:
        near *= 2
    assert n % near == 0 and (n // near) & (n // near - 1) == 0
    return n // near, near


def flips(i, n):
    steps, bit = [], 1
    while bit < n:
        steps.append((bit, bit - 2 * bit * lax.rem(i // bit, 2)))
        bit *= 2
    peers = []
    for d in range(n):
        peer = i
        for bit, step in steps:
            if d & bit:
                peer = peer + step
        peers.append(peer)
    return peers


def kernel(far, near, n_pts, pts_ref, cen_ref, out_ref, en_ref,
           x_ref, w_ref, cur_ref, low_ref, sq_ref, block_top, whole, stat, got,
           p_send, f_recv, n_recv, s_send, s_recv, c_send, c_recv,
           in_sem, cen_sem):
    steps, own, dim = pts_ref.shape
    k_loc = cen_ref.shape[0]
    n_blk = k_loc // ROWS
    n_cen = far * near
    width = near * own
    cols = width // LANES
    groups = far * cols
    unroll = groups * n_blk <= UNROLL
    cen = lax.axis_index("cen")
    p = lax.axis_index("pts")
    a = cen // near
    b = lax.rem(cen, near)
    a_flip = flips(a, far)
    b_flip = flips(b, near)
    pts_peers = [lax.rem(p + d, n_pts) for d in range(1, n_pts)]

    barrier = pltpu.get_barrier_semaphore()
    for peer in a_flip[1:]:
        pl.semaphore_signal(barrier, inc=1, device_id={"cen": peer * near + b}, device_id_type=MESH)
    for peer in b_flip[1:]:
        pl.semaphore_signal(barrier, inc=1, device_id={"cen": a * near + peer}, device_id_type=MESH)
    for peer in pts_peers:
        pl.semaphore_signal(barrier, inc=1, device_id={"pts": peer}, device_id_type=MESH)

    def rows_of(blk):
        return pl.ds(blk * ROWS if isinstance(blk, int) else pl.multiple_of(blk * ROWS, ROWS), ROWS)

    def each(body):
        if unroll:
            for blk in range(n_blk):
                body(blk)
        else:
            pl.loop(0, n_blk)(body)

    def folded(body, value):
        if unroll:
            for blk in range(n_blk):
                value = body(blk, value)
            return value
        return lax.fori_loop(0, n_blk, body, value)

    def lowered(value):
        sq = jnp.sum(value * value, axis=1, keepdims=True) * (1.0 / TEMPER)
        return (value * (2.0 / TEMPER)).astype(jnp.bfloat16), sq

    def cen_copy(blk):
        rows = rows_of(blk)
        return pltpu.make_async_copy(cen_ref.at[rows, :], cur_ref.at[rows, :], cen_sem.at[blk])

    def chunk(s, d):
        return x_ref.at[s, pl.ds(pl.multiple_of(d * width + b * own, own), own), :]

    def pts_copy(s):
        return pltpu.make_async_copy(pts_ref.at[s], chunk(s, 0), in_sem.at[s])

    def landed(ref, sem):
        pltpu.make_async_remote_copy(
            src_ref=ref, dst_ref=ref, send_sem=sem, recv_sem=sem,
            device_id={"cen": cen}, device_id_type=MESH).wait_recv()

    def sent(ref, sem):
        pltpu.make_async_remote_copy(
            src_ref=ref, dst_ref=ref, send_sem=sem, recv_sem=sem,
            device_id={"cen": cen}, device_id_type=MESH).wait_send()

    def chunks(s, n):
        return x_ref.at[s, pl.ds(0, n * own), :]

    def far_copy(s, d):
        return pltpu.make_async_remote_copy(
            src_ref=pts_ref.at[s], dst_ref=chunk(s, d),
            send_sem=p_send.at[s], recv_sem=f_recv.at[d if s == 0 else far + s - 1],
            device_id={"cen": a_flip[d] * near + b}, device_id_type=MESH)

    def near_copy(s, d, e):
        return pltpu.make_async_remote_copy(
            src_ref=pts_ref.at[s] if d == 0 else chunk(s, d), dst_ref=chunk(s, d),
            send_sem=p_send.at[s], recv_sem=n_recv.at[min(d, 1) if s == 0 else s + 1],
            device_id={"cen": a * near + b_flip[e]}, device_id_type=MESH)

    def send_near(s, d):
        for e in reversed(range(1, near)):
            near_copy(s, d, e).start()

    def send_far(s):
        for d in reversed(range(1, far)):
            far_copy(s, d).start()

    def forward(s):
        if s > 0:
            send_near(s, 0)
            landed(chunks(s, far - 1), f_recv.at[far + s - 1])
        for d in range(1, far):
            if s == 0:
                landed(chunk(s, d), f_recv.at[d])
            send_near(s, d)

    def stat_copy(s, d):
        return pltpu.make_async_remote_copy(
            src_ref=stat.at[s, cen], dst_ref=stat.at[s, cen],
            send_sem=s_send.at[s], recv_sem=s_recv.at[s],
            device_id={"cen": a_flip[d // near] * near + b_flip[d % near]}, device_id_type=MESH)

    def sums_copy(s, d, blk):
        return pltpu.make_async_remote_copy(
            src_ref=got.at[s, p, blk], dst_ref=got.at[s, p, blk],
            send_sem=c_send.at[s], recv_sem=c_recv.at[s, blk],
            device_id={"pts": pts_peers[d - 1]}, device_id_type=MESH)

    for s in range(steps):
        pts_copy(s).start()

    @pl.loop(0, n_blk)
    def _(blk):
        cen_copy(blk).start()

    with jax.named_scope("entry"):
        pl.semaphore_wait(barrier, (far - 1) + (near - 1) + (n_pts - 1))
        send_far(0)
        send_near(0, 0)

    with jax.named_scope("prepare"):
        @pl.loop(0, n_blk)
        def _(blk):
            cen_copy(blk).wait()
            rows = rows_of(blk)
            low_ref[rows, :], sq = lowered(cur_ref[rows, :])
            sq_ref[rows, :] = jnp.broadcast_to(sq, (ROWS, LANES))

    with jax.named_scope("forward0"):
        forward(0)
    if steps > 1:
        send_far(1)
    for s in range(steps):
        pts_copy(s).wait()

    def combine(pairs):
        best = functools.reduce(jnp.maximum, [top for top, _ in pairs])
        return best, sum(jnp.exp(top - best) * total for top, total in pairs)

    def keep(s, d, top, total):
        part = top + jnp.log(total)
        for j in range(cols):
            lanes = slice(j * LANES, (j + 1) * LANES)
            stat[s, cen, pl.ds(a_flip[d] * cols + j, 1), :] = part[:, lanes]

    def weights_of(d, n, size):
        xs = x_ref[0, d * width:(d + n) * width, :]
        pairs = []
        for k in range(0, k_loc, size):
            rows = slice(k, k + size)
            logits = lax.dot_general(
                low_ref[rows, :], xs, (((1,), (1,)), ((), ())),
                preferred_element_type=jnp.float32)
            logits = logits - jnp.concatenate([sq_ref[rows, :]] * (n * cols), axis=1)
            top = jnp.max(logits, axis=0, keepdims=True)
            weights = jnp.exp(logits - top)
            w_ref[rows, d * width:(d + n) * width] = weights
            block_top[k // size, 0:1, d * width:(d + n) * width] = top
            pairs.append((top, jnp.sum(weights, axis=0, keepdims=True)))
        top, total = combine(pairs)
        for i in range(n):
            lanes = slice(i * width, (i + 1) * width)
            keep(0, d + i, top[:, lanes], total[:, lanes])

    with jax.named_scope("group0"):
        landed(chunks(0, near - 1), n_recv.at[0])
        weights_of(0, 1, BLOCK)
    with jax.named_scope("arrive"):
        landed(chunks(0, (far - 1) * (near - 1)), n_recv.at[1])
    with jax.named_scope("group3"):
        weights_of(1, far - 1, BLOCK)

    for s in range(steps):
        for d in reversed(range(1, n_cen)):
            stat_copy(s, d).start()
        if s + 1 < steps:
            with jax.named_scope("forward1"):
                forward(s + 1)
            if s + 2 < steps:
                send_far(s + 2)
        with jax.named_scope("stats" + str(s)):
            landed(stat.at[s, pl.ds(0, n_cen - 1)], s_recv.at[s])
        parts = stat[s]
        best = jnp.max(parts, axis=0)
        energy = best + jnp.log(jnp.sum(jnp.exp(parts - best[None]), axis=0))
        whole[...] = energy
        for g in range(groups):
            en_ref[s:s + 1, g * LANES:(g + 1) * LANES] = energy[g:g + 1, :]
        energy = jnp.concatenate(
            [whole[pl.ds(a_flip[d] * cols + j, 1), :] for d in range(far) for j in range(cols)], axis=1)

        def scale_of(blk):
            n = ROWS // BLOCK
            rows = [block_top[blk * n + i, 0:1, :] if s == 0 else block_top[0, 0:1, :] for i in range(n)]
            return [jnp.exp(row - energy) for row in rows]

        def gather(blk):
            rows = rows_of(blk)
            weights = w_ref[rows, :]
            resp = jnp.concatenate(
                [weights[i * BLOCK:(i + 1) * BLOCK, :] * scale for i, scale in enumerate(scale_of(blk))], axis=0)
            part = resp[:, :LANES]
            for g in range(1, groups):
                part = part + resp[:, g * LANES:(g + 1) * LANES]
            count = jnp.sum(jnp.transpose(part), axis=0, keepdims=True)
            sums = lax.dot_general(
                resp.astype(jnp.bfloat16), x_ref[s], (((1,), (0,)), ((), ())),
                preferred_element_type=jnp.float32)
            got[s, p, blk, :ROWS, :] = sums
            got[s, p, blk, ROWS:ROWS + 1, :] = count
            for d in range(1, n_pts):
                sums_copy(s, d, blk).start()

        with jax.named_scope("sums" + str(s)):
            each(gather)

        if s + 1 < steps:
            with jax.named_scope("points" + str(s + 1)):
                landed(chunks(s + 1, far * (near - 1)), n_recv.at[s + 2])

        def finish(blk, top):
            rows = rows_of(blk)
            landed(got.at[s, pl.ds(0, n_pts - 1), blk], c_recv.at[s, blk])
            sums = got[s, 0, blk, :ROWS, :]
            count = got[s, 0, blk, ROWS:ROWS + 1, :]
            for i in range(1, n_pts):
                sums = sums + got[s, i, blk, :ROWS, :]
                count = count + got[s, i, blk, ROWS:ROWS + 1, :]
            column = jnp.transpose(jnp.broadcast_to(1.0 / (1.0 + count), (LANES, ROWS)))
            column = jnp.concatenate([column] * (dim // LANES), axis=1)
            value = (cur_ref[rows, :] + sums) * column
            if s + 1 == steps:
                out_ref[rows, :] = value
                return top
            cur_ref[rows, :] = value
            low, sq = lowered(value)
            logits = lax.dot_general(
                low, x_ref[s + 1], (((1,), (1,)), ((), ())),
                preferred_element_type=jnp.float32) - sq
            w_ref[rows, :] = logits
            return jnp.maximum(top, jnp.max(logits, axis=0, keepdims=True))

        def weigh(top, blk, total):
            rows = rows_of(blk)
            weights = jnp.exp(w_ref[rows, :] - top)
            w_ref[rows, :] = weights
            return total + jnp.sum(weights, axis=0, keepdims=True)

        with jax.named_scope("finish" + str(s)):
            top = folded(finish, jnp.full((1, groups * LANES), -jnp.inf, jnp.float32))
        if s + 1 < steps:
            with jax.named_scope("weigh"):
                total = folded(functools.partial(weigh, top), jnp.zeros_like(top))
            block_top[0, 0:1, :] = top
            for d in range(far):
                lanes = slice(d * width, (d + 1) * width)
                keep(s + 1, d, top[:, lanes], total[:, lanes])

    with jax.named_scope("drain"):
        for s in range(steps):
            sent(chunks(s, n_cen - 1), p_send.at[s])
            sent(stat.at[s, pl.ds(0, n_cen - 1)], s_send.at[s])
            sent(got.at[s, pl.ds(0, n_pts - 1)], c_send.at[s])


def emit(value_ref, part_ref, out_ref, en_ref, sems):
    copies = [pltpu.make_async_copy(value_ref, out_ref, sems.at[0]),
              pltpu.make_async_copy(part_ref, en_ref, sems.at[1])]
    for copy in copies:
        copy.start()
    for copy in copies:
        copy.wait()


def on_device(far, near, n_pts, points, centroids):
    steps, own, dim = points.shape
    k_loc = centroids.shape[0]
    n_blk = k_loc // ROWS
    n_cen = far * near
    batch = n_cen * own
    groups = batch // LANES
    vmem = pl.BlockSpec(memory_space=pltpu.VMEM)
    dma = pltpu.SemaphoreType.DMA
    value, energy = pl.pallas_call(
        functools.partial(kernel, far, near, n_pts),
        out_shape=(pltpu.VMEM((k_loc, dim), jnp.float32),
                   pltpu.VMEM((steps, batch), jnp.float32)),
        in_specs=[pl.BlockSpec(memory_space=pl.ANY)] * 2,
        out_specs=(vmem, vmem),
        scratch_shapes=[
            pltpu.VMEM((steps, batch, dim), jnp.bfloat16),
            pltpu.VMEM((k_loc, batch), jnp.float32),
            pltpu.VMEM((k_loc, dim), jnp.float32),
            pltpu.VMEM((k_loc, dim), jnp.bfloat16),
            pltpu.VMEM((k_loc, LANES), jnp.float32),
            pltpu.VMEM((k_loc // BLOCK, 8, batch), jnp.float32),
            pltpu.VMEM((groups, LANES), jnp.float32),
            pltpu.VMEM((steps, n_cen, groups, LANES), jnp.float32),
            pltpu.VMEM((steps, n_pts, n_blk, ROWS + 8, dim), jnp.float32),
            dma((steps,)),
            dma((far + steps - 1,)),
            dma((steps + 1,)),
            dma((steps,)),
            dma((steps,)),
            dma((steps,)),
            dma((steps, n_blk)),
            dma((steps,)),
            dma((n_blk,)),
        ],
        compiler_params=pltpu.CompilerParams(
            collective_id=0, has_side_effects=True, vmem_limit_bytes=58 * 1024 * 1024),
    )(points, centroids)
    return pl.pallas_call(
        emit,
        out_shape=(jax.ShapeDtypeStruct((k_loc, dim), jnp.float32),
                   jax.ShapeDtypeStruct((steps, batch), jnp.float32)),
        in_specs=[vmem, vmem],
        out_specs=[pl.BlockSpec(memory_space=pltpu.HBM)] * 2,
        scratch_shapes=[dma((2,))],
        compiler_params=pltpu.CompilerParams(vmem_limit_bytes=1024 * 1024),
    )(value, energy)


def solution(mesh):
    far, near = split(mesh.shape["cen"])
    placed = (P(None, ("pts", "cen"), None), P("cen", None))
    return jax.shard_map(
        functools.partial(on_device, far, near, mesh.shape["pts"]),
        mesh=mesh,
        in_specs=placed,
        out_specs=(P("cen", None), P(None, "pts")),
        check_vma=False,
    )
```

```python
import functools

import jax
import jax.numpy as jnp
from jax import lax
from jax.experimental import pallas as pl
from jax.experimental.pallas import tpu as pltpu
from jax.sharding import PartitionSpec as P

TEMPER = 32.0
MESH = pl.DeviceIdType.MESH
LANES = 128
ROWS = 256
BLOCK = 128
UNROLL = 32


def split(n):
    near = 1
    while near * near * 4 <= n:
        near *= 2
    assert n % near == 0 and (n // near) & (n // near - 1) == 0
    return n // near, near


def flips(i, n):
    steps, bit = [], 1
    while bit < n:
        steps.append((bit, bit - 2 * bit * lax.rem(i // bit, 2)))
        bit *= 2
    peers = []
    for d in range(n):
        peer = i
        for bit, step in steps:
            if d & bit:
                peer = peer + step
        peers.append(peer)
    return peers


def kernel(far, near, n_pts, pts_ref, cen_ref, out_ref, en_ref,
           x_ref, w_ref, cur_ref, low_ref, sq_ref, block_top, whole, stat,
           p_send, f_recv, n_recv, s_send, s_recv, c_send, c_recv,
           in_sem, cen_sem, *rest):
    pair = n_pts == 2
    acc_ref, part_ref = rest if pair else (None, None)
    got = None if pair else rest[0]
    steps, own, dim = pts_ref.shape
    k_loc = cen_ref.shape[0]
    n_blk = k_loc // ROWS
    n_cen = far * near
    width = near * own
    cols = width // LANES
    groups = far * cols
    unroll = groups * n_blk <= UNROLL
    cen = lax.axis_index("cen")
    p = lax.axis_index("pts")
    a = cen // near
    b = lax.rem(cen, near)
    a_flip = flips(a, far)
    b_flip = flips(b, near)
    pts_peers = [lax.rem(p + d, n_pts) for d in range(1, n_pts)]

    barrier = pltpu.get_barrier_semaphore()
    for peer in a_flip[1:]:
        pl.semaphore_signal(barrier, inc=1, device_id={"cen": peer * near + b}, device_id_type=MESH)
    for peer in b_flip[1:]:
        pl.semaphore_signal(barrier, inc=1, device_id={"cen": a * near + peer}, device_id_type=MESH)
    for peer in pts_peers:
        pl.semaphore_signal(barrier, inc=1, device_id={"pts": peer}, device_id_type=MESH)

    def rows_of(blk):
        return pl.ds(blk * ROWS if isinstance(blk, int) else pl.multiple_of(blk * ROWS, ROWS), ROWS)

    def each(body):
        if unroll:
            for blk in range(n_blk):
                body(blk)
        else:
            pl.loop(0, n_blk)(body)

    def folded(body, value):
        if unroll:
            for blk in range(n_blk):
                value = body(blk, value)
            return value
        return lax.fori_loop(0, n_blk, body, value)

    def lowered(value):
        sq = jnp.sum(value * value, axis=1, keepdims=True) * (1.0 / TEMPER)
        return (value * (2.0 / TEMPER)).astype(jnp.bfloat16), sq

    def cen_copy(blk):
        rows = rows_of(blk)
        return pltpu.make_async_copy(cen_ref.at[rows, :], cur_ref.at[rows, :], cen_sem.at[blk])

    def chunk(s, d):
        return x_ref.at[s, 0, pl.ds(pl.multiple_of(d * width + b * own, own), own), :]

    def pts_copy(s):
        return pltpu.make_async_copy(pts_ref.at[s], chunk(s, 0), in_sem.at[s])

    def landed(ref, sem):
        pltpu.make_async_remote_copy(
            src_ref=ref, dst_ref=ref, send_sem=sem, recv_sem=sem,
            device_id={"cen": cen}, device_id_type=MESH).wait_recv()

    def sent(ref, sem):
        pltpu.make_async_remote_copy(
            src_ref=ref, dst_ref=ref, send_sem=sem, recv_sem=sem,
            device_id={"cen": cen}, device_id_type=MESH).wait_send()

    def chunks(s, n):
        return x_ref.at[s, 0, pl.ds(0, n * own), :]

    def far_copy(s, d):
        return pltpu.make_async_remote_copy(
            src_ref=pts_ref.at[s], dst_ref=chunk(s, d),
            send_sem=p_send.at[s], recv_sem=f_recv.at[d if s == 0 else far + s - 1],
            device_id={"cen": a_flip[d] * near + b}, device_id_type=MESH)

    def near_copy(s, d, e):
        return pltpu.make_async_remote_copy(
            src_ref=pts_ref.at[s] if d == 0 else chunk(s, d), dst_ref=chunk(s, d),
            send_sem=p_send.at[s], recv_sem=n_recv.at[min(d, 1) if s == 0 else s + 1],
            device_id={"cen": a * near + b_flip[e]}, device_id_type=MESH)

    def send_near(s, d):
        for e in reversed(range(1, near)):
            near_copy(s, d, e).start()

    def send_far(s):
        for d in reversed(range(1, far)):
            far_copy(s, d).start()

    def forward(s):
        if s > 0:
            send_near(s, 0)
            landed(chunks(s, far - 1), f_recv.at[far + s - 1])
        for d in range(1, far):
            if s == 0:
                landed(chunk(s, d), f_recv.at[d])
            send_near(s, d)

    def stat_copy(s, d):
        return pltpu.make_async_remote_copy(
            src_ref=stat.at[s, cen], dst_ref=stat.at[s, cen],
            send_sem=s_send.at[s], recv_sem=s_recv.at[s],
            device_id={"cen": a_flip[d // near] * near + b_flip[d % near]}, device_id_type=MESH)

    def sums_copy(s, d, blk):
        return pltpu.make_async_remote_copy(
            src_ref=got.at[s, p, blk], dst_ref=got.at[s, p, blk],
            send_sem=c_send.at[s], recv_sem=c_recv.at[s * n_blk + blk],
            device_id={"pts": pts_peers[d - 1]}, device_id_type=MESH)

    def pair_copy(ref, i):
        return pltpu.make_async_remote_copy(
            src_ref=ref.at[0], dst_ref=ref.at[1], send_sem=c_send.at[i], recv_sem=c_recv.at[i],
            device_id={"pts": pts_peers[0]}, device_id_type=MESH)

    for s in range(steps):
        pts_copy(s).start()

    @pl.loop(0, n_blk)
    def _(blk):
        cen_copy(blk).start()

    with jax.named_scope("entry"):
        pl.semaphore_wait(barrier, (far - 1) + (near - 1) + (n_pts - 1))
        send_far(0)
        send_near(0, 0)

    with jax.named_scope("prepare"):
        @pl.loop(0, n_blk)
        def _(blk):
            cen_copy(blk).wait()
            rows = rows_of(blk)
            low_ref[rows, :], sq = lowered(cur_ref[rows, :])
            sq_ref[rows, :] = jnp.broadcast_to(sq, (ROWS, LANES))

    with jax.named_scope("forward0"):
        forward(0)
    if steps > 1:
        send_far(1)
    for s in range(steps):
        pts_copy(s).wait()

    def combine(pairs):
        best = functools.reduce(jnp.maximum, [top for top, _ in pairs])
        return best, sum(jnp.exp(top - best) * total for top, total in pairs)

    def keep(s, d, top, total):
        part = top + jnp.log(total)
        for j in range(cols):
            lanes = slice(j * LANES, (j + 1) * LANES)
            stat[s, cen, pl.ds(a_flip[d] * cols + j, 1), :] = part[:, lanes]

    def logits_of(low, sq, xs):
        logits = lax.dot_general(
            low, xs, (((1,), (1,)), ((), ())), preferred_element_type=jnp.float32)
        if sq.shape[1] > 1:
            sq = jnp.concatenate([sq] * (logits.shape[1] // LANES), axis=1)
        return logits - sq

    def weights_of(q, d, n):
        lanes = slice(d * width, (d + n) * width)
        xs = x_ref[0, q, lanes, :]
        pairs = []
        for k in range(0, k_loc, BLOCK):
            rows = slice(k, k + BLOCK)
            logits = logits_of(low_ref[rows, :], sq_ref[rows, :], xs)
            top = jnp.max(logits, axis=0, keepdims=True)
            weights = jnp.exp(logits - top)
            w_ref[q, rows, lanes] = weights
            block_top[q, k // BLOCK, 0:1, lanes] = top
            pairs.append((top, jnp.sum(weights, axis=0, keepdims=True)))
        return combine(pairs)

    def first_weights(d, n):
        top, total = weights_of(0, d, n)
        for i in range(n):
            lanes = slice(i * width, (i + 1) * width)
            keep(0, d + i, top[:, lanes], total[:, lanes])

    def weigh(q, top, blk, total):
        rows = rows_of(blk)
        weights = jnp.exp(w_ref[q, rows, :] - top)
        w_ref[q, rows, :] = weights
        return total + jnp.sum(weights, axis=0, keepdims=True)

    def resp_of(s, q, energy, blk):
        rows = rows_of(blk)
        weights = w_ref[q, rows, :]
        if s > 0:
            return weights * jnp.exp(block_top[q, 0, 0:1, :] - energy)
        n = ROWS // BLOCK
        return jnp.concatenate(
            [weights[i * BLOCK:(i + 1) * BLOCK, :] * jnp.exp(block_top[q, blk * n + i, 0:1, :] - energy)
             for i in range(n)], axis=0)

    def lanes_of(resp):
        part = resp[:, :LANES]
        for g in range(1, groups):
            part = part + resp[:, g * LANES:(g + 1) * LANES]
        return part

    def sums_of(s, q, resp):
        return lax.dot_general(
            resp.astype(jnp.bfloat16), x_ref[s, q], (((1,), (0,)), ((), ())),
            preferred_element_type=jnp.float32)

    def energy_of(s, q):
        return jnp.concatenate(
            [whole[s, q, pl.ds(a_flip[d] * cols + j, 1), :] for d in range(far) for j in range(cols)], axis=1)

    lowest = jnp.full((1, groups * LANES), -jnp.inf, jnp.float32)
    with jax.named_scope("group0"):
        landed(chunks(0, near - 1), n_recv.at[0])
        first_weights(0, 1)
    with jax.named_scope("arrive"):
        landed(chunks(0, (far - 1) * (near - 1)), n_recv.at[1])
        if pair:
            pair_copy(x_ref.at[0], 0).start()
    with jax.named_scope("group3"):
        first_weights(1, far - 1)

    for s in range(steps):
        for d in reversed(range(1, n_cen)):
            stat_copy(s, d).start()
        if s + 1 < steps:
            with jax.named_scope("forward1"):
                forward(s + 1)
            if s + 2 < steps:
                send_far(s + 2)
        if pair:
            with jax.named_scope("other" + str(s)):
                landed(x_ref.at[s, 1], c_recv.at[2 * s])
                if s == 0:
                    weights_of(1, 0, far)
                else:
                    def logits_block(blk, top):
                        rows = rows_of(blk)
                        logits = logits_of(low_ref[rows, :], sq_ref[rows, :], x_ref[s, 1])
                        w_ref[1, rows, :] = logits
                        return jnp.maximum(top, jnp.max(logits, axis=0, keepdims=True))

                    top = folded(logits_block, lowest)
                    folded(functools.partial(weigh, 1, top), jnp.zeros_like(top))
                    block_top[1, 0, 0:1, :] = top
        with jax.named_scope("stats" + str(s)):
            landed(stat.at[s, pl.ds(0, n_cen - 1)], s_recv.at[s])
        parts = stat[s]
        best = jnp.max(parts, axis=0)
        energy = best + jnp.log(jnp.sum(jnp.exp(parts - best[None]), axis=0))
        whole[s, 0] = energy
        if pair:
            pair_copy(whole.at[s], 2 * s + 1).start()
        for g in range(groups):
            en_ref[s:s + 1, g * LANES:(g + 1) * LANES] = energy[g:g + 1, :]
        energy = energy_of(s, 0)

        def updated(blk, sums, column):
            rows = rows_of(blk)
            value = (cur_ref[rows, :] + sums) * column
            if s + 1 == steps:
                out_ref[rows, :] = value
                return None
            cur_ref[rows, :] = value
            low, sq = lowered(value)
            if pair:
                low_ref[rows, :] = low
                sq_ref[rows, :] = jnp.broadcast_to(sq, (ROWS, LANES))
            logits = logits_of(low, sq, x_ref[s + 1, 0])
            w_ref[0, rows, :] = logits
            return jnp.max(logits, axis=0, keepdims=True)

        def arrived_next():
            if s + 1 < steps:
                with jax.named_scope("points" + str(s + 1)):
                    landed(chunks(s + 1, far * (near - 1)), n_recv.at[s + 2])
                    if pair:
                        pair_copy(x_ref.at[s + 1], 2 * s + 2).start()

        if pair:
            def own_sums(blk):
                rows = rows_of(blk)
                resp = resp_of(s, 0, energy, blk)
                part_ref[rows, :] = lanes_of(resp)
                acc_ref[rows, :] = sums_of(s, 0, resp)

            with jax.named_scope("sums" + str(s)):
                each(own_sums)
            arrived_next()
            with jax.named_scope("whole" + str(s)):
                landed(whole.at[s, 1], c_recv.at[2 * s + 1])
            other = energy_of(s, 1)

            def finish(blk, top):
                rows = rows_of(blk)
                resp = resp_of(s, 1, other, blk)
                count = jnp.sum(part_ref[rows, :] + lanes_of(resp), axis=1, keepdims=True)
                sums = acc_ref[rows, :] + sums_of(s, 1, resp)
                best = updated(blk, sums, 1.0 / (1.0 + count))
                return top if best is None else jnp.maximum(top, best)
        else:
            def gather(blk):
                resp = resp_of(s, 0, energy, blk)
                count = jnp.sum(jnp.transpose(lanes_of(resp)), axis=0, keepdims=True)
                got[s, p, blk, :ROWS, :] = sums_of(s, 0, resp)
                got[s, p, blk, ROWS:ROWS + 1, :] = count
                for d in range(1, n_pts):
                    sums_copy(s, d, blk).start()

            with jax.named_scope("sums" + str(s)):
                each(gather)
            arrived_next()

            def finish(blk, top):
                if n_pts > 1:
                    landed(got.at[s, pl.ds(0, n_pts - 1), blk], c_recv.at[s * n_blk + blk])
                sums = got[s, 0, blk, :ROWS, :]
                count = got[s, 0, blk, ROWS:ROWS + 1, :]
                for i in range(1, n_pts):
                    sums = sums + got[s, i, blk, :ROWS, :]
                    count = count + got[s, i, blk, ROWS:ROWS + 1, :]
                column = jnp.transpose(jnp.broadcast_to(1.0 / (1.0 + count), (LANES, ROWS)))
                best = updated(blk, sums, jnp.concatenate([column] * (dim // LANES), axis=1))
                return top if best is None else jnp.maximum(top, best)

        with jax.named_scope("finish" + str(s)):
            top = folded(finish, lowest)
        if s + 1 < steps:
            with jax.named_scope("weigh"):
                total = folded(functools.partial(weigh, 0, top), jnp.zeros_like(top))
            block_top[0, 0, 0:1, :] = top
            for d in range(far):
                lanes = slice(d * width, (d + 1) * width)
                keep(s + 1, d, top[:, lanes], total[:, lanes])

    with jax.named_scope("drain"):
        for s in range(steps):
            sent(chunks(s, n_cen - 1), p_send.at[s])
            sent(stat.at[s, pl.ds(0, n_cen - 1)], s_send.at[s])
            if pair:
                sent(x_ref.at[s, 0], c_send.at[2 * s])
                sent(whole.at[s, 0], c_send.at[2 * s + 1])
            elif n_pts > 1:
                sent(got.at[s, pl.ds(0, n_pts - 1)], c_send.at[s])


def emit(value_ref, part_ref, out_ref, en_ref, sems):
    copies = [pltpu.make_async_copy(value_ref, out_ref, sems.at[0]),
              pltpu.make_async_copy(part_ref, en_ref, sems.at[1])]
    for copy in copies:
        copy.start()
    for copy in copies:
        copy.wait()


def on_device(far, near, n_pts, points, centroids):
    steps, own, dim = points.shape
    k_loc = centroids.shape[0]
    n_blk = k_loc // ROWS
    n_cen = far * near
    batch = n_cen * own
    groups = batch // LANES
    sides = 2 if n_pts == 2 else 1
    vmem = pl.BlockSpec(memory_space=pltpu.VMEM)
    dma = pltpu.SemaphoreType.DMA
    value, energy = pl.pallas_call(
        functools.partial(kernel, far, near, n_pts),
        out_shape=(pltpu.VMEM((k_loc, dim), jnp.float32),
                   pltpu.VMEM((steps, batch), jnp.float32)),
        in_specs=[pl.BlockSpec(memory_space=pl.ANY)] * 2,
        out_specs=(vmem, vmem),
        scratch_shapes=[
            pltpu.VMEM((steps, sides, batch, dim), jnp.bfloat16),
            pltpu.VMEM((sides, k_loc, batch), jnp.float32),
            pltpu.VMEM((k_loc, dim), jnp.float32),
            pltpu.VMEM((k_loc, dim), jnp.bfloat16),
            pltpu.VMEM((k_loc, LANES), jnp.float32),
            pltpu.VMEM((sides, k_loc // BLOCK, 8, batch), jnp.float32),
            pltpu.VMEM((steps, sides, groups, LANES), jnp.float32),
            pltpu.VMEM((steps, n_cen, groups, LANES), jnp.float32),
            dma((steps,)),
            dma((far + steps - 1,)),
            dma((steps + 1,)),
            dma((steps,)),
            dma((steps,)),
            dma((2 * steps,)),
            dma((2 * steps if n_pts == 2 else steps * n_blk,)),
            dma((steps,)),
            dma((n_blk,)),
        ] + ([
            pltpu.VMEM((k_loc, dim), jnp.float32),
            pltpu.VMEM((k_loc, LANES), jnp.float32),
        ] if n_pts == 2 else [
            pltpu.VMEM((steps, n_pts, n_blk, ROWS + 8, dim), jnp.float32),
        ]),
        compiler_params=pltpu.CompilerParams(
            collective_id=0, has_side_effects=True, vmem_limit_bytes=58 * 1024 * 1024),
    )(points, centroids)
    return pl.pallas_call(
        emit,
        out_shape=(jax.ShapeDtypeStruct((k_loc, dim), jnp.float32),
                   jax.ShapeDtypeStruct((steps, batch), jnp.float32)),
        in_specs=[vmem, vmem],
        out_specs=[pl.BlockSpec(memory_space=pltpu.HBM)] * 2,
        scratch_shapes=[dma((2,))],
        compiler_params=pltpu.CompilerParams(vmem_limit_bytes=1024 * 1024),
    )(value, energy)


def solution(mesh):
    far, near = split(mesh.shape["cen"])
    placed = (P(None, ("pts", "cen"), None), P("cen", None))
    return jax.shard_map(
        functools.partial(on_device, far, near, mesh.shape["pts"]),
        mesh=mesh,
        in_specs=placed,
        out_specs=(P("cen", None), P(None, "pts")),
        check_vma=False,
    )
```

```python
import functools

import jax
import jax.numpy as jnp
from jax import lax
from jax.experimental import pallas as pl
from jax.experimental.pallas import tpu as pltpu
from jax.sharding import PartitionSpec as P

TEMPER = 32.0
MESH = pl.DeviceIdType.MESH
LANES = 128
ROWS = 256
BLOCK = 128
UNROLL = 32


def split(n):
    near = 1
    while near * near * 4 <= n:
        near *= 2
    assert n % near == 0 and (n // near) & (n // near - 1) == 0
    return n // near, near


def flips(i, n):
    steps, bit = [], 1
    while bit < n:
        steps.append((bit, bit - 2 * bit * lax.rem(lax.div(i, bit), 2)))
        bit *= 2
    peers = []
    for d in range(n):
        peer = i
        for bit, step in steps:
            if d & bit:
                peer = peer + step
        peers.append(peer)
    return peers


def kernel(far, near, n_pts, pts_ref, cen_ref, out_ref, en_ref,
           x_ref, w_ref, cur_ref, low_ref, sq_ref, block_top, whole, stat,
           p_send, f_recv, n_recv, s_send, s_recv, c_send, c_recv,
           in_sem, cen_sem, *rest):
    pair = n_pts == 2
    acc_ref, part_ref = rest if pair else (None, None)
    got = None if pair else rest[0]
    steps, own, dim = pts_ref.shape
    k_loc = cen_ref.shape[0]
    n_blk = k_loc // ROWS
    n_cen = far * near
    width = near * own
    cols = width // LANES
    groups = far * cols
    unroll = groups * n_blk <= UNROLL
    cen = lax.axis_index("cen")
    p = lax.axis_index("pts")
    a = lax.div(cen, near)
    b = lax.rem(cen, near)
    a_flip = flips(a, far)
    b_flip = flips(b, near)
    pts_peers = [lax.rem(p + d, n_pts) for d in range(1, n_pts)]

    barrier = pltpu.get_barrier_semaphore()
    for peer in a_flip[1:]:
        pl.semaphore_signal(barrier, inc=1, device_id={"cen": peer * near + b}, device_id_type=MESH)
    for peer in b_flip[1:]:
        pl.semaphore_signal(barrier, inc=1, device_id={"cen": a * near + peer}, device_id_type=MESH)
    for peer in pts_peers:
        pl.semaphore_signal(barrier, inc=1, device_id={"pts": peer}, device_id_type=MESH)

    def rows_of(blk):
        return pl.ds(blk * ROWS if isinstance(blk, int) else pl.multiple_of(blk * ROWS, ROWS), ROWS)

    def each(body):
        if unroll:
            for blk in range(n_blk):
                body(blk)
        else:
            pl.loop(0, n_blk)(body)

    def folded(body, value):
        if unroll:
            for blk in range(n_blk):
                value = body(blk, value)
            return value
        return lax.fori_loop(0, n_blk, body, value)

    def lowered(value):
        sq = jnp.sum(value * value, axis=1, keepdims=True) * (1.0 / TEMPER)
        return (value * (2.0 / TEMPER)).astype(jnp.bfloat16), sq

    def cen_copy(blk):
        rows = rows_of(blk)
        return pltpu.make_async_copy(cen_ref.at[rows, :], cur_ref.at[rows, :], cen_sem.at[blk])

    def chunk(s, d):
        return x_ref.at[s, 0, pl.ds(pl.multiple_of(d * width + b * own, own), own), :]

    def pts_copy(s):
        return pltpu.make_async_copy(pts_ref.at[s], chunk(s, 0), in_sem.at[s])

    def landed(ref, sem):
        pltpu.make_async_remote_copy(
            src_ref=ref, dst_ref=ref, send_sem=sem, recv_sem=sem,
            device_id={"cen": cen}, device_id_type=MESH).wait_recv()

    def sent(ref, sem):
        pltpu.make_async_remote_copy(
            src_ref=ref, dst_ref=ref, send_sem=sem, recv_sem=sem,
            device_id={"cen": cen}, device_id_type=MESH).wait_send()

    def chunks(s, n):
        return x_ref.at[s, 0, pl.ds(0, n * own), :]

    def far_copy(s, d):
        return pltpu.make_async_remote_copy(
            src_ref=chunk(s, 0), dst_ref=chunk(s, d),
            send_sem=p_send.at[s], recv_sem=f_recv.at[d if s == 0 else far + s - 1],
            device_id={"cen": a_flip[d] * near + b}, device_id_type=MESH)

    def near_copy(s, d, e):
        return pltpu.make_async_remote_copy(
            src_ref=chunk(s, d), dst_ref=chunk(s, d),
            send_sem=p_send.at[s], recv_sem=n_recv.at[min(d, 1) if s == 0 else s + 1],
            device_id={"cen": a * near + b_flip[e]}, device_id_type=MESH)

    def send_near(s, d):
        for e in reversed(range(1, near)):
            near_copy(s, d, e).start()

    def send_far(s):
        for d in reversed(range(1, far)):
            far_copy(s, d).start()

    def forward(s):
        if s > 0:
            send_near(s, 0)
            landed(chunks(s, far - 1), f_recv.at[far + s - 1])
        for d in range(1, far):
            if s == 0:
                landed(chunk(s, d), f_recv.at[d])
            send_near(s, d)

    def stat_copy(s, d):
        return pltpu.make_async_remote_copy(
            src_ref=stat.at[s, cen], dst_ref=stat.at[s, cen],
            send_sem=s_send.at[s], recv_sem=s_recv.at[s],
            device_id={"cen": a_flip[d // near] * near + b_flip[d % near]}, device_id_type=MESH)

    def cross_copy(s, d):
        return pltpu.make_async_remote_copy(
            src_ref=stat.at[s, cen], dst_ref=stat.at[s, n_cen + cen],
            send_sem=s_send.at[s], recv_sem=s_recv.at[steps + s],
            device_id={"cen": a_flip[d // near] * near + b_flip[d % near], "pts": pts_peers[0]},
            device_id_type=MESH)

    def crossed(s):
        return pair and s > 0

    def total_of(s, q):
        parts = stat[s, q * n_cen:(q + 1) * n_cen]
        best = jnp.max(parts, axis=0)
        return best + jnp.log(jnp.sum(jnp.exp(parts - best[None]), axis=0))

    def sums_copy(s, d, blk):
        return pltpu.make_async_remote_copy(
            src_ref=got.at[s, p, blk], dst_ref=got.at[s, p, blk],
            send_sem=c_send.at[s], recv_sem=c_recv.at[s * n_blk + blk],
            device_id={"pts": pts_peers[d - 1]}, device_id_type=MESH)

    def pair_copy(ref, i):
        return pltpu.make_async_remote_copy(
            src_ref=ref.at[0], dst_ref=ref.at[1], send_sem=c_send.at[i], recv_sem=c_recv.at[i],
            device_id={"pts": pts_peers[0]}, device_id_type=MESH)

    for s in range(steps):
        pts_copy(s).start()

    @pl.loop(0, n_blk)
    def _(blk):
        cen_copy(blk).start()

    with jax.named_scope("own"):
        for s in range(steps):
            pts_copy(s).wait()
    with jax.named_scope("entry"):
        pl.semaphore_wait(barrier, (far - 1) + (near - 1) + (n_pts - 1))
        send_far(0)
        send_near(0, 0)

    with jax.named_scope("prepare"):
        @pl.loop(0, n_blk)
        def _(blk):
            cen_copy(blk).wait()
            rows = rows_of(blk)
            low_ref[rows, :], sq = lowered(cur_ref[rows, :])
            sq_ref[rows, :] = jnp.broadcast_to(sq, (ROWS, LANES))

    with jax.named_scope("forward0"):
        forward(0)
    if steps > 1:
        send_far(1)

    def combine(pairs):
        best = functools.reduce(jnp.maximum, [top for top, _ in pairs])
        return best, sum(jnp.exp(top - best) * total for top, total in pairs)

    def keep(s, d, top, total):
        part = top + jnp.log(total)
        for j in range(cols):
            lanes = slice(j * LANES, (j + 1) * LANES)
            stat[s, cen, pl.ds(a_flip[d] * cols + j, 1), :] = part[:, lanes]

    def logits_of(low, sq, xs):
        logits = lax.dot_general(
            low, xs, (((1,), (1,)), ((), ())), preferred_element_type=jnp.float32)
        if sq.shape[1] > 1:
            sq = jnp.concatenate([sq] * (logits.shape[1] // LANES), axis=1)
        return logits - sq

    def weights_of(q, d, n):
        lanes = slice(d * width, (d + n) * width)
        xs = x_ref[0, q, lanes, :]
        pairs = []
        for k in range(0, k_loc, BLOCK):
            rows = slice(k, k + BLOCK)
            logits = logits_of(low_ref[rows, :], sq_ref[rows, :], xs)
            top = jnp.max(logits, axis=0, keepdims=True)
            weights = jnp.exp(logits - top)
            w_ref[q, rows, lanes] = weights
            block_top[q, k // BLOCK, 0:1, lanes] = top
            pairs.append((top, jnp.sum(weights, axis=0, keepdims=True)))
        return combine(pairs)

    def first_weights(d, n):
        top, total = weights_of(0, d, n)
        for i in range(n):
            lanes = slice(i * width, (i + 1) * width)
            keep(0, d + i, top[:, lanes], total[:, lanes])

    def weigh(q, top, blk, total):
        rows = rows_of(blk)
        weights = jnp.exp(w_ref[q, rows, :] - top)
        w_ref[q, rows, :] = weights
        return total + jnp.sum(weights, axis=0, keepdims=True)

    def resp_of(s, q, energy, blk):
        rows = rows_of(blk)
        weights = w_ref[q, rows, :]
        if s > 0:
            return weights * jnp.exp(block_top[q, 0, 0:1, :] - energy)
        n = ROWS // BLOCK
        return jnp.concatenate(
            [weights[i * BLOCK:(i + 1) * BLOCK, :] * jnp.exp(block_top[q, blk * n + i, 0:1, :] - energy)
             for i in range(n)], axis=0)

    def lanes_of(resp):
        part = resp[:, :LANES]
        for g in range(1, groups):
            part = part + resp[:, g * LANES:(g + 1) * LANES]
        return part

    def sums_of(s, q, resp):
        return lax.dot_general(
            resp.astype(jnp.bfloat16), x_ref[s, q], (((1,), (0,)), ((), ())),
            preferred_element_type=jnp.float32)

    def energy_of(s, q):
        return jnp.concatenate(
            [whole[s, q, pl.ds(a_flip[d] * cols + j, 1), :] for d in range(far) for j in range(cols)], axis=1)

    lowest = jnp.full((1, groups * LANES), -jnp.inf, jnp.float32)
    with jax.named_scope("group0"):
        landed(chunks(0, near - 1), n_recv.at[0])
        first_weights(0, 1)
    with jax.named_scope("arrive"):
        landed(chunks(0, (far - 1) * (near - 1)), n_recv.at[1])
        if pair:
            pair_copy(x_ref.at[0], 0).start()
    with jax.named_scope("group3"):
        first_weights(1, far - 1)

    for s in range(steps):
        for d in reversed(range(1, n_cen)):
            stat_copy(s, d).start()
        if crossed(s):
            for d in reversed(range(n_cen)):
                cross_copy(s, d).start()
        if s + 1 < steps:
            with jax.named_scope("forward1"):
                forward(s + 1)
            if s + 2 < steps:
                send_far(s + 2)
        if pair:
            with jax.named_scope("other" + str(s)):
                landed(x_ref.at[s, 1], c_recv.at[2 * s])
                if s == 0:
                    weights_of(1, 0, far)
                else:
                    def logits_block(blk, top):
                        rows = rows_of(blk)
                        logits = logits_of(low_ref[rows, :], sq_ref[rows, :], x_ref[s, 1])
                        w_ref[1, rows, :] = logits
                        return jnp.maximum(top, jnp.max(logits, axis=0, keepdims=True))

                    top = folded(logits_block, lowest)
                    folded(functools.partial(weigh, 1, top), jnp.zeros_like(top))
                    block_top[1, 0, 0:1, :] = top
        with jax.named_scope("stats" + str(s)):
            landed(stat.at[s, pl.ds(0, n_cen - 1)], s_recv.at[s])
        energy = total_of(s, 0)
        whole[s, 0] = energy
        if pair and not crossed(s):
            pair_copy(whole.at[s], 2 * s + 1).start()
        for g in range(groups):
            en_ref[s:s + 1, g * LANES:(g + 1) * LANES] = energy[g:g + 1, :]
        energy = energy_of(s, 0)

        def updated(blk, sums, column):
            rows = rows_of(blk)
            value = (cur_ref[rows, :] + sums) * column
            if s + 1 == steps:
                out_ref[rows, :] = value
                return None
            cur_ref[rows, :] = value
            low, sq = lowered(value)
            if pair:
                low_ref[rows, :] = low
                sq_ref[rows, :] = jnp.broadcast_to(sq, (ROWS, LANES))
            logits = logits_of(low, sq, x_ref[s + 1, 0])
            w_ref[0, rows, :] = logits
            return jnp.max(logits, axis=0, keepdims=True)

        def arrived_next():
            if s + 1 < steps:
                with jax.named_scope("points" + str(s + 1)):
                    landed(chunks(s + 1, far * (near - 1)), n_recv.at[s + 2])
                    if pair:
                        pair_copy(x_ref.at[s + 1], 2 * s + 2).start()

        if pair:
            def own_sums(blk):
                rows = rows_of(blk)
                resp = resp_of(s, 0, energy, blk)
                part_ref[rows, :] = lanes_of(resp)
                acc_ref[rows, :] = sums_of(s, 0, resp)

            with jax.named_scope("sums" + str(s)):
                each(own_sums)
            arrived_next()
            with jax.named_scope("whole" + str(s)):
                if crossed(s):
                    landed(stat.at[s, pl.ds(0, n_cen)], s_recv.at[steps + s])
                    whole[s, 1] = total_of(s, 1)
                else:
                    landed(whole.at[s, 1], c_recv.at[2 * s + 1])
            other = energy_of(s, 1)

            def other_sums(blk):
                rows = rows_of(blk)
                resp = resp_of(s, 1, other, blk)
                count = jnp.sum(part_ref[rows, :] + lanes_of(resp), axis=1, keepdims=True)
                part_ref[rows, :] = jnp.broadcast_to(1.0 / (1.0 + count), (ROWS, LANES))
                acc_ref[rows, :] = acc_ref[rows, :] + sums_of(s, 1, resp)

            if s + 1 < steps:
                with jax.named_scope("othersums" + str(s)):
                    each(other_sums)

            def finish(blk, top):
                rows = rows_of(blk)
                if s + 1 == steps:
                    resp = resp_of(s, 1, other, blk)
                    count = jnp.sum(part_ref[rows, :] + lanes_of(resp), axis=1, keepdims=True)
                    updated(blk, acc_ref[rows, :] + sums_of(s, 1, resp), 1.0 / (1.0 + count))
                    return top
                column = jnp.concatenate([part_ref[rows, :]] * (dim // LANES), axis=1)
                best = updated(blk, acc_ref[rows, :], column)
                return top if best is None else jnp.maximum(top, best)
        else:
            def gather(blk):
                resp = resp_of(s, 0, energy, blk)
                count = jnp.sum(jnp.transpose(lanes_of(resp)), axis=0, keepdims=True)
                got[s, p, blk, :ROWS, :] = sums_of(s, 0, resp)
                got[s, p, blk, ROWS:ROWS + 1, :] = count
                for d in range(1, n_pts):
                    sums_copy(s, d, blk).start()

            with jax.named_scope("sums" + str(s)):
                each(gather)
            arrived_next()

            def finish(blk, top):
                if n_pts > 1:
                    landed(got.at[s, pl.ds(0, n_pts - 1), blk], c_recv.at[s * n_blk + blk])
                sums = got[s, 0, blk, :ROWS, :]
                count = got[s, 0, blk, ROWS:ROWS + 1, :]
                for i in range(1, n_pts):
                    sums = sums + got[s, i, blk, :ROWS, :]
                    count = count + got[s, i, blk, ROWS:ROWS + 1, :]
                column = jnp.transpose(jnp.broadcast_to(1.0 / (1.0 + count), (LANES, ROWS)))
                best = updated(blk, sums, jnp.concatenate([column] * (dim // LANES), axis=1))
                return top if best is None else jnp.maximum(top, best)

        with jax.named_scope("finish" + str(s)):
            top = folded(finish, lowest)
        if s + 1 < steps:
            with jax.named_scope("weigh"):
                total = folded(functools.partial(weigh, 0, top), jnp.zeros_like(top))
            block_top[0, 0, 0:1, :] = top
            for d in range(far):
                lanes = slice(d * width, (d + 1) * width)
                keep(s + 1, d, top[:, lanes], total[:, lanes])

    with jax.named_scope("drain"):
        for s in range(steps):
            sent(chunks(s, n_cen - 1), p_send.at[s])
            sent(stat.at[s, pl.ds(0, (2 * n_cen if crossed(s) else n_cen) - 1)], s_send.at[s])
            if pair:
                sent(x_ref.at[s, 0], c_send.at[2 * s])
                if not crossed(s):
                    sent(whole.at[s, 0], c_send.at[2 * s + 1])
            elif n_pts > 1:
                sent(got.at[s, pl.ds(0, n_pts - 1)], c_send.at[s])


def emit(value_ref, part_ref, out_ref, en_ref, sems):
    copies = [pltpu.make_async_copy(value_ref, out_ref, sems.at[0]),
              pltpu.make_async_copy(part_ref, en_ref, sems.at[1])]
    for copy in copies:
        copy.start()
    for copy in copies:
        copy.wait()


def on_device(far, near, n_pts, points, centroids):
    steps, own, dim = points.shape
    k_loc = centroids.shape[0]
    n_blk = k_loc // ROWS
    n_cen = far * near
    batch = n_cen * own
    groups = batch // LANES
    sides = 2 if n_pts == 2 else 1
    vmem = pl.BlockSpec(memory_space=pltpu.VMEM)
    dma = pltpu.SemaphoreType.DMA
    value, energy = pl.pallas_call(
        functools.partial(kernel, far, near, n_pts),
        out_shape=(pltpu.VMEM((k_loc, dim), jnp.float32),
                   pltpu.VMEM((steps, batch), jnp.float32)),
        in_specs=[pl.BlockSpec(memory_space=pl.ANY)] * 2,
        out_specs=(vmem, vmem),
        scratch_shapes=[
            pltpu.VMEM((steps, sides, batch, dim), jnp.bfloat16),
            pltpu.VMEM((sides, k_loc, batch), jnp.float32),
            pltpu.VMEM((k_loc, dim), jnp.float32),
            pltpu.VMEM((k_loc, dim), jnp.bfloat16),
            pltpu.VMEM((k_loc, LANES), jnp.float32),
            pltpu.VMEM((sides, k_loc // BLOCK, 8, batch), jnp.float32),
            pltpu.VMEM((steps, sides, groups, LANES), jnp.float32),
            pltpu.VMEM((steps, sides * n_cen, groups, LANES), jnp.float32),
            dma((steps,)),
            dma((far + steps - 1,)),
            dma((steps + 1,)),
            dma((steps,)),
            dma((sides * steps,)),
            dma((2 * steps,)),
            dma((2 * steps if n_pts == 2 else steps * n_blk,)),
            dma((steps,)),
            dma((n_blk,)),
        ] + ([
            pltpu.VMEM((k_loc, dim), jnp.float32),
            pltpu.VMEM((k_loc, LANES), jnp.float32),
        ] if n_pts == 2 else [
            pltpu.VMEM((steps, n_pts, n_blk, ROWS + 8, dim), jnp.float32),
        ]),
        compiler_params=pltpu.CompilerParams(
            collective_id=0, has_side_effects=True, vmem_limit_bytes=58 * 1024 * 1024),
    )(points, centroids)
    return pl.pallas_call(
        emit,
        out_shape=(jax.ShapeDtypeStruct((k_loc, dim), jnp.float32),
                   jax.ShapeDtypeStruct((steps, batch), jnp.float32)),
        in_specs=[vmem, vmem],
        out_specs=[pl.BlockSpec(memory_space=pltpu.HBM)] * 2,
        scratch_shapes=[dma((2,))],
        compiler_params=pltpu.CompilerParams(vmem_limit_bytes=1024 * 1024),
    )(value, energy)


def solution(mesh):
    far, near = split(mesh.shape["cen"])
    placed = (P(None, ("pts", "cen"), None), P("cen", None))
    return jax.shard_map(
        functools.partial(on_device, far, near, mesh.shape["pts"]),
        mesh=mesh,
        in_specs=placed,
        out_specs=(P("cen", None), P(None, "pts")),
        check_vma=False,
    )
```

```python
import functools

import jax
import jax.numpy as jnp
from jax import lax
from jax.experimental import pallas as pl
from jax.experimental.pallas import tpu as pltpu
from jax.sharding import PartitionSpec as P

TEMPER = 32.0
MESH = pl.DeviceIdType.MESH
LANES = 128
ROWS = 256
BLOCK = 128
UNROLL = 32
HUB = 1


def split(n):
    near = 1
    while near * near * 4 <= n:
        near *= 2
    assert n % near == 0 and (n // near) & (n // near - 1) == 0
    return n // near, near


def flips(i, n):
    steps, bit = [], 1
    while bit < n:
        steps.append((bit, bit - 2 * bit * lax.rem(lax.div(i, bit), 2)))
        bit *= 2
    peers = []
    for d in range(n):
        peer = i
        for bit, step in steps:
            if d & bit:
                peer = peer + step
        peers.append(peer)
    return peers


def kernel(far, near, n_pts, pts_ref, cen_ref, out_ref, en_ref,
           x_ref, w_ref, cur_ref, low_ref, sq_ref, block_top, whole, stat,
           p_send, f_recv, n_recv, s_send, s_recv, c_send, c_recv,
           in_sem, cen_sem, *rest):
    pair = n_pts == 2
    acc_ref, part_ref, hub_ref, h_send = rest if pair else (None,) * 4
    got = None if pair else rest[0]
    steps, own, dim = pts_ref.shape
    k_loc = cen_ref.shape[0]
    n_blk = k_loc // ROWS
    n_cen = far * near
    width = near * own
    cols = width // LANES
    groups = far * cols
    unroll = groups * n_blk <= UNROLL
    cen = lax.axis_index("cen")
    p = lax.axis_index("pts")
    a = lax.div(cen, near)
    b = lax.rem(cen, near)
    a_flip = flips(a, far)
    b_flip = flips(b, near)
    pts_peers = [lax.rem(p + d, n_pts) for d in range(1, n_pts)]

    barrier = pltpu.get_barrier_semaphore()
    for peer in a_flip[1:]:
        pl.semaphore_signal(barrier, inc=1, device_id={"cen": peer * near + b}, device_id_type=MESH)
    for peer in b_flip[1:]:
        pl.semaphore_signal(barrier, inc=1, device_id={"cen": a * near + peer}, device_id_type=MESH)
    for peer in pts_peers:
        pl.semaphore_signal(barrier, inc=1, device_id={"pts": peer}, device_id_type=MESH)
    if pair:
        @pl.when(p == HUB)
        def _():
            for peer in a_flip[1:]:
                pl.semaphore_signal(
                    barrier, inc=1, device_id={"cen": peer * near + b, "pts": 1 - HUB}, device_id_type=MESH)

        @pl.when(p != HUB)
        def _():
            for peer in b_flip[1:]:
                pl.semaphore_signal(
                    barrier, inc=1, device_id={"cen": a * near + peer, "pts": HUB}, device_id_type=MESH)

    def rows_of(blk):
        return pl.ds(blk * ROWS if isinstance(blk, int) else pl.multiple_of(blk * ROWS, ROWS), ROWS)

    def each(body):
        if unroll:
            for blk in range(n_blk):
                body(blk)
        else:
            pl.loop(0, n_blk)(body)

    def folded(body, value):
        if unroll:
            for blk in range(n_blk):
                value = body(blk, value)
            return value
        return lax.fori_loop(0, n_blk, body, value)

    def lowered(value):
        sq = jnp.sum(value * value, axis=1, keepdims=True) * (1.0 / TEMPER)
        return (value * (2.0 / TEMPER)).astype(jnp.bfloat16), sq

    def cen_copy(blk):
        rows = rows_of(blk)
        return pltpu.make_async_copy(cen_ref.at[rows, :], cur_ref.at[rows, :], cen_sem.at[blk])

    def chunk(s, d):
        return x_ref.at[s, 0, pl.ds(pl.multiple_of(d * width + b * own, own), own), :]

    def pts_copy(s):
        return pltpu.make_async_copy(pts_ref.at[s], chunk(s, 0), in_sem.at[s])

    def landed(ref, sem):
        pltpu.make_async_remote_copy(
            src_ref=ref, dst_ref=ref, send_sem=sem, recv_sem=sem,
            device_id={"cen": cen}, device_id_type=MESH).wait_recv()

    def sent(ref, sem):
        pltpu.make_async_remote_copy(
            src_ref=ref, dst_ref=ref, send_sem=sem, recv_sem=sem,
            device_id={"cen": cen}, device_id_type=MESH).wait_send()

    def chunks(s, n):
        return x_ref.at[s, 0, pl.ds(0, n * own), :]

    def far_copy(s, d):
        return pltpu.make_async_remote_copy(
            src_ref=chunk(s, 0), dst_ref=chunk(s, d),
            send_sem=p_send.at[s], recv_sem=f_recv.at[d if s == 0 else far + s - 1],
            device_id={"cen": a_flip[d] * near + b}, device_id_type=MESH)

    def near_copy(s, d, e):
        return pltpu.make_async_remote_copy(
            src_ref=chunk(s, d), dst_ref=chunk(s, d),
            send_sem=p_send.at[s], recv_sem=n_recv.at[min(d, 1) if s == 0 else s + 1],
            device_id={"cen": a * near + b_flip[e]}, device_id_type=MESH)

    def hub_copy(d):
        return pltpu.make_async_remote_copy(
            src_ref=chunk(0, 0), dst_ref=hub_ref.at[d],
            send_sem=p_send.at[0], recv_sem=f_recv.at[far + steps - 1 + d],
            device_id={"cen": a_flip[d] * near + b, "pts": HUB}, device_id_type=MESH)

    def relay_copy(d, e):
        return pltpu.make_async_remote_copy(
            src_ref=hub_ref.at[d], dst_ref=chunk(0, d),
            send_sem=h_send.at[0], recv_sem=n_recv.at[1],
            device_id={"cen": a * near + b_flip[e], "pts": 1 - HUB}, device_id_type=MESH)

    def relay():
        for d in range(1, far):
            landed(hub_ref.at[d], f_recv.at[far + steps - 1 + d])
            for e in reversed(range(near)):
                relay_copy(d, e).start()

    def send_near(s, d):
        for e in reversed(range(1, near)):
            near_copy(s, d, e).start()

    def send_far(s):
        for d in reversed(range(1, far)):
            far_copy(s, d).start()

    def forward(s):
        if s > 0:
            send_near(s, 0)
            landed(chunks(s, far - 1), f_recv.at[far + s - 1])
        for d in range(1, far):
            if s == 0:
                landed(chunk(s, d), f_recv.at[d])
            send_near(s, d)

    def stat_copy(s, d):
        return pltpu.make_async_remote_copy(
            src_ref=stat.at[s, cen], dst_ref=stat.at[s, cen],
            send_sem=s_send.at[s], recv_sem=s_recv.at[s],
            device_id={"cen": a_flip[d // near] * near + b_flip[d % near]}, device_id_type=MESH)

    def cross_copy(s, d):
        return pltpu.make_async_remote_copy(
            src_ref=stat.at[s, cen], dst_ref=stat.at[s, n_cen + cen],
            send_sem=s_send.at[s], recv_sem=s_recv.at[steps + s],
            device_id={"cen": a_flip[d // near] * near + b_flip[d % near], "pts": pts_peers[0]},
            device_id_type=MESH)

    def crossed(s):
        return pair and s > 0

    def total_of(s, q):
        parts = stat[s, q * n_cen:(q + 1) * n_cen]
        best = jnp.max(parts, axis=0)
        return best + jnp.log(jnp.sum(jnp.exp(parts - best[None]), axis=0))

    def sums_copy(s, d, blk):
        return pltpu.make_async_remote_copy(
            src_ref=got.at[s, p, blk], dst_ref=got.at[s, p, blk],
            send_sem=c_send.at[s], recv_sem=c_recv.at[s * n_blk + blk],
            device_id={"pts": pts_peers[d - 1]}, device_id_type=MESH)

    def pair_copy(ref, i):
        return pltpu.make_async_remote_copy(
            src_ref=ref.at[0], dst_ref=ref.at[1], send_sem=c_send.at[i], recv_sem=c_recv.at[i],
            device_id={"pts": pts_peers[0]}, device_id_type=MESH)

    for s in range(steps):
        pts_copy(s).start()

    @pl.loop(0, n_blk)
    def _(blk):
        cen_copy(blk).start()

    with jax.named_scope("own"):
        for s in range(steps):
            pts_copy(s).wait()
    with jax.named_scope("entry"):
        extra = jnp.where(p == HUB, near - 1, far - 1) if pair else 0
        pl.semaphore_wait(barrier, (far - 1) + (near - 1) + (n_pts - 1) + extra)
        if pair:
            @pl.when(p == HUB)
            def _():
                send_far(0)

            @pl.when(p != HUB)
            def _():
                for d in reversed(range(1, far)):
                    hub_copy(d).start()
        else:
            send_far(0)
        send_near(0, 0)

    with jax.named_scope("prepare"):
        @pl.loop(0, n_blk)
        def _(blk):
            cen_copy(blk).wait()
            rows = rows_of(blk)
            low_ref[rows, :], sq = lowered(cur_ref[rows, :])
            sq_ref[rows, :] = jnp.broadcast_to(sq, (ROWS, LANES))

    with jax.named_scope("forward0"):
        if pair:
            @pl.when(p == HUB)
            def _():
                forward(0)
                relay()
        else:
            forward(0)
    if steps > 1:
        send_far(1)

    def combine(pairs):
        best = functools.reduce(jnp.maximum, [top for top, _ in pairs])
        return best, sum(jnp.exp(top - best) * total for top, total in pairs)

    def keep(s, d, top, total):
        part = top + jnp.log(total)
        for j in range(cols):
            lanes = slice(j * LANES, (j + 1) * LANES)
            stat[s, cen, pl.ds(a_flip[d] * cols + j, 1), :] = part[:, lanes]

    def logits_of(low, sq, xs):
        logits = lax.dot_general(
            low, xs, (((1,), (1,)), ((), ())), preferred_element_type=jnp.float32)
        if sq.shape[1] > 1:
            sq = jnp.concatenate([sq] * (logits.shape[1] // LANES), axis=1)
        return logits - sq

    def weights_of(q, d, n):
        lanes = slice(d * width, (d + n) * width)
        xs = x_ref[0, q, lanes, :]
        pairs = []
        for k in range(0, k_loc, BLOCK):
            rows = slice(k, k + BLOCK)
            logits = logits_of(low_ref[rows, :], sq_ref[rows, :], xs)
            top = jnp.max(logits, axis=0, keepdims=True)
            weights = jnp.exp(logits - top)
            w_ref[q, rows, lanes] = weights
            block_top[q, k // BLOCK, 0:1, lanes] = top
            pairs.append((top, jnp.sum(weights, axis=0, keepdims=True)))
        return combine(pairs)

    def first_weights(d, n):
        top, total = weights_of(0, d, n)
        for i in range(n):
            lanes = slice(i * width, (i + 1) * width)
            keep(0, d + i, top[:, lanes], total[:, lanes])

    def weigh(q, top, blk, total):
        rows = rows_of(blk)
        weights = jnp.exp(w_ref[q, rows, :] - top)
        w_ref[q, rows, :] = weights
        return total + jnp.sum(weights, axis=0, keepdims=True)

    def resp_of(s, q, energy, blk):
        rows = rows_of(blk)
        weights = w_ref[q, rows, :]
        if s > 0:
            return weights * jnp.exp(block_top[q, 0, 0:1, :] - energy)
        n = ROWS // BLOCK
        return jnp.concatenate(
            [weights[i * BLOCK:(i + 1) * BLOCK, :] * jnp.exp(block_top[q, blk * n + i, 0:1, :] - energy)
             for i in range(n)], axis=0)

    def lanes_of(resp):
        part = resp[:, :LANES]
        for g in range(1, groups):
            part = part + resp[:, g * LANES:(g + 1) * LANES]
        return part

    def sums_of(s, q, resp):
        return lax.dot_general(
            resp.astype(jnp.bfloat16), x_ref[s, q], (((1,), (0,)), ((), ())),
            preferred_element_type=jnp.float32)

    def energy_of(s, q):
        return jnp.concatenate(
            [whole[s, q, pl.ds(a_flip[d] * cols + j, 1), :] for d in range(far) for j in range(cols)], axis=1)

    lowest = jnp.full((1, groups * LANES), -jnp.inf, jnp.float32)
    with jax.named_scope("group0"):
        landed(chunks(0, near - 1), n_recv.at[0])
        first_weights(0, 1)
    with jax.named_scope("arrive"):
        if pair:
            @pl.when(p == HUB)
            def _():
                landed(chunks(0, (far - 1) * (near - 1)), n_recv.at[1])

            @pl.when(p != HUB)
            def _():
                landed(chunks(0, (far - 1) * near), n_recv.at[1])
        else:
            landed(chunks(0, (far - 1) * (near - 1)), n_recv.at[1])
        if pair:
            pair_copy(x_ref.at[0], 0).start()
    with jax.named_scope("group3"):
        first_weights(1, far - 1)

    for s in range(steps):
        for d in reversed(range(1, n_cen)):
            stat_copy(s, d).start()
        if crossed(s):
            for d in reversed(range(n_cen)):
                cross_copy(s, d).start()
        if s + 1 < steps:
            with jax.named_scope("forward1"):
                forward(s + 1)
            if s + 2 < steps:
                send_far(s + 2)
        if pair:
            with jax.named_scope("other" + str(s)):
                landed(x_ref.at[s, 1], c_recv.at[2 * s])
                if s == 0:
                    weights_of(1, 0, far)
                else:
                    def logits_block(blk, top):
                        rows = rows_of(blk)
                        logits = logits_of(low_ref[rows, :], sq_ref[rows, :], x_ref[s, 1])
                        w_ref[1, rows, :] = logits
                        return jnp.maximum(top, jnp.max(logits, axis=0, keepdims=True))

                    top = folded(logits_block, lowest)
                    folded(functools.partial(weigh, 1, top), jnp.zeros_like(top))
                    block_top[1, 0, 0:1, :] = top
        with jax.named_scope("stats" + str(s)):
            landed(stat.at[s, pl.ds(0, n_cen - 1)], s_recv.at[s])
        energy = total_of(s, 0)
        whole[s, 0] = energy
        if pair and not crossed(s):
            pair_copy(whole.at[s], 2 * s + 1).start()
        for g in range(groups):
            en_ref[s:s + 1, g * LANES:(g + 1) * LANES] = energy[g:g + 1, :]
        energy = energy_of(s, 0)

        def updated(blk, sums, column):
            rows = rows_of(blk)
            value = (cur_ref[rows, :] + sums) * column
            if s + 1 == steps:
                out_ref[rows, :] = value
                return None
            cur_ref[rows, :] = value
            low, sq = lowered(value)
            if pair:
                low_ref[rows, :] = low
                sq_ref[rows, :] = jnp.broadcast_to(sq, (ROWS, LANES))
            logits = logits_of(low, sq, x_ref[s + 1, 0])
            w_ref[0, rows, :] = logits
            return jnp.max(logits, axis=0, keepdims=True)

        def arrived_next():
            if s + 1 < steps:
                with jax.named_scope("points" + str(s + 1)):
                    landed(chunks(s + 1, far * (near - 1)), n_recv.at[s + 2])
                    if pair:
                        pair_copy(x_ref.at[s + 1], 2 * s + 2).start()

        if pair:
            def own_sums(blk):
                rows = rows_of(blk)
                resp = resp_of(s, 0, energy, blk)
                part_ref[rows, :] = lanes_of(resp)
                acc_ref[rows, :] = sums_of(s, 0, resp)

            with jax.named_scope("sums" + str(s)):
                each(own_sums)
            arrived_next()
            with jax.named_scope("whole" + str(s)):
                if crossed(s):
                    landed(stat.at[s, pl.ds(0, n_cen)], s_recv.at[steps + s])
                    whole[s, 1] = total_of(s, 1)
                else:
                    landed(whole.at[s, 1], c_recv.at[2 * s + 1])
            other = energy_of(s, 1)

            def other_sums(blk):
                rows = rows_of(blk)
                resp = resp_of(s, 1, other, blk)
                count = jnp.sum(part_ref[rows, :] + lanes_of(resp), axis=1, keepdims=True)
                part_ref[rows, :] = jnp.broadcast_to(1.0 / (1.0 + count), (ROWS, LANES))
                acc_ref[rows, :] = acc_ref[rows, :] + sums_of(s, 1, resp)

            if s + 1 < steps:
                with jax.named_scope("othersums" + str(s)):
                    each(other_sums)

            def finish(blk, top):
                rows = rows_of(blk)
                if s + 1 == steps:
                    resp = resp_of(s, 1, other, blk)
                    count = jnp.sum(part_ref[rows, :] + lanes_of(resp), axis=1, keepdims=True)
                    updated(blk, acc_ref[rows, :] + sums_of(s, 1, resp), 1.0 / (1.0 + count))
                    return top
                column = jnp.concatenate([part_ref[rows, :]] * (dim // LANES), axis=1)
                best = updated(blk, acc_ref[rows, :], column)
                return top if best is None else jnp.maximum(top, best)
        else:
            def gather(blk):
                resp = resp_of(s, 0, energy, blk)
                count = jnp.sum(jnp.transpose(lanes_of(resp)), axis=0, keepdims=True)
                got[s, p, blk, :ROWS, :] = sums_of(s, 0, resp)
                got[s, p, blk, ROWS:ROWS + 1, :] = count
                for d in range(1, n_pts):
                    sums_copy(s, d, blk).start()

            with jax.named_scope("sums" + str(s)):
                each(gather)
            arrived_next()

            def finish(blk, top):
                if n_pts > 1:
                    landed(got.at[s, pl.ds(0, n_pts - 1), blk], c_recv.at[s * n_blk + blk])
                sums = got[s, 0, blk, :ROWS, :]
                count = got[s, 0, blk, ROWS:ROWS + 1, :]
                for i in range(1, n_pts):
                    sums = sums + got[s, i, blk, :ROWS, :]
                    count = count + got[s, i, blk, ROWS:ROWS + 1, :]
                column = jnp.transpose(jnp.broadcast_to(1.0 / (1.0 + count), (LANES, ROWS)))
                best = updated(blk, sums, jnp.concatenate([column] * (dim // LANES), axis=1))
                return top if best is None else jnp.maximum(top, best)

        with jax.named_scope("finish" + str(s)):
            top = folded(finish, lowest)
        if s + 1 < steps:
            with jax.named_scope("weigh"):
                total = folded(functools.partial(weigh, 0, top), jnp.zeros_like(top))
            block_top[0, 0, 0:1, :] = top
            for d in range(far):
                lanes = slice(d * width, (d + 1) * width)
                keep(s + 1, d, top[:, lanes], total[:, lanes])

    with jax.named_scope("drain"):
        for s in range(steps):
            if pair and s == 0:
                @pl.when(p == HUB)
                def _():
                    sent(chunks(0, n_cen - 1), p_send.at[0])
                    sent(chunks(0, (far - 1) * near), h_send.at[0])

                @pl.when(p != HUB)
                def _():
                    sent(chunks(0, far + near - 2), p_send.at[0])
            else:
                sent(chunks(s, n_cen - 1), p_send.at[s])
            sent(stat.at[s, pl.ds(0, (2 * n_cen if crossed(s) else n_cen) - 1)], s_send.at[s])
            if pair:
                sent(x_ref.at[s, 0], c_send.at[2 * s])
                if not crossed(s):
                    sent(whole.at[s, 0], c_send.at[2 * s + 1])
            elif n_pts > 1:
                sent(got.at[s, pl.ds(0, n_pts - 1)], c_send.at[s])


def emit(value_ref, part_ref, out_ref, en_ref, sems):
    copies = [pltpu.make_async_copy(value_ref, out_ref, sems.at[0]),
              pltpu.make_async_copy(part_ref, en_ref, sems.at[1])]
    for copy in copies:
        copy.start()
    for copy in copies:
        copy.wait()


def on_device(far, near, n_pts, points, centroids):
    steps, own, dim = points.shape
    k_loc = centroids.shape[0]
    n_blk = k_loc // ROWS
    n_cen = far * near
    batch = n_cen * own
    groups = batch // LANES
    sides = 2 if n_pts == 2 else 1
    vmem = pl.BlockSpec(memory_space=pltpu.VMEM)
    dma = pltpu.SemaphoreType.DMA
    value, energy = pl.pallas_call(
        functools.partial(kernel, far, near, n_pts),
        out_shape=(pltpu.VMEM((k_loc, dim), jnp.float32),
                   pltpu.VMEM((steps, batch), jnp.float32)),
        in_specs=[pl.BlockSpec(memory_space=pl.ANY)] * 2,
        out_specs=(vmem, vmem),
        scratch_shapes=[
            pltpu.VMEM((steps, sides, batch, dim), jnp.bfloat16),
            pltpu.VMEM((sides, k_loc, batch), jnp.float32),
            pltpu.VMEM((k_loc, dim), jnp.float32),
            pltpu.VMEM((k_loc, dim), jnp.bfloat16),
            pltpu.VMEM((k_loc, LANES), jnp.float32),
            pltpu.VMEM((sides, k_loc // BLOCK, 8, batch), jnp.float32),
            pltpu.VMEM((steps, sides, groups, LANES), jnp.float32),
            pltpu.VMEM((steps, sides * n_cen, groups, LANES), jnp.float32),
            dma((steps,)),
            dma((2 * far + steps - 1,)),
            dma((steps + 1,)),
            dma((steps,)),
            dma((sides * steps,)),
            dma((2 * steps,)),
            dma((2 * steps if n_pts == 2 else steps * n_blk,)),
            dma((steps,)),
            dma((n_blk,)),
        ] + ([
            pltpu.VMEM((k_loc, dim), jnp.float32),
            pltpu.VMEM((k_loc, LANES), jnp.float32),
            pltpu.VMEM((far, own, dim), jnp.bfloat16),
            dma((1,)),
        ] if n_pts == 2 else [
            pltpu.VMEM((steps, n_pts, n_blk, ROWS + 8, dim), jnp.float32),
        ]),
        compiler_params=pltpu.CompilerParams(
            collective_id=0, has_side_effects=True, vmem_limit_bytes=58 * 1024 * 1024),
    )(points, centroids)
    return pl.pallas_call(
        emit,
        out_shape=(jax.ShapeDtypeStruct((k_loc, dim), jnp.float32),
                   jax.ShapeDtypeStruct((steps, batch), jnp.float32)),
        in_specs=[vmem, vmem],
        out_specs=[pl.BlockSpec(memory_space=pltpu.HBM)] * 2,
        scratch_shapes=[dma((2,))],
        compiler_params=pltpu.CompilerParams(vmem_limit_bytes=1024 * 1024),
    )(value, energy)


def solution(mesh):
    far, near = split(mesh.shape["cen"])
    placed = (P(None, ("pts", "cen"), None), P("cen", None))
    return jax.shard_map(
        functools.partial(on_device, far, near, mesh.shape["pts"]),
        mesh=mesh,
        in_specs=placed,
        out_specs=(P("cen", None), P(None, "pts")),
        check_vma=False,
    )
```
